128 devices in a mesh: freq: 4 (over z), tile: 32 (over y, x, core).
Axes of the slice: x: 4, y: 4, z: 4, core: 2. Of those that a mesh axis runs over, the one named last changes fastest.
Arguments:
- traces: bfloat16 [32768, 1024], P('tile'), may hold values from -6 to 6
- bins: int32 [32768], P('tile'), may hold values from 0 to 196607, as said below
- counts: int32 [32], P('tile'), may hold values from 512 to 1024, as said below
- delay: float32 [2, 384, 512], P(None, 'tile'), may hold values from 0.02 to 0.06
- coeffs: float32 [2, 9, 256], P(None, None, 'freq'), may hold values from -1.4 to 1.4
Outputs:
- image: float32 [2, 384, 512], P(None, 'tile', 'freq')
The draws below stay inside these ranges and needn't reach their ends.
Inputs may be any that keep to these rules, and one draw needn't show every extreme that they name: `bins`: only the first counts[o] trace slots of owner o are used; among them at most 80 fall in the 6144 cells of any one tile (rows x * 12 to x * 12 + 11), and in every draw some tile receives exactly 80 live traces from every owner. `counts`: some owner has all 1024 slots live.
All inputs are finite; a program needn't handle non-finite values.
Results may differ from the reference program's by a relative error of at most 0.0037.
Values may be sent and summed in bfloat16 or wider, within the bound.
No kernel may reach another device: no remote copies, remote signals or barrier semaphores. Data moves between devices by JAX's collectives and lax.ppermute only.
A program may use at most 320 MiB of HBM per device.

```python
import math
import jax
import jax.numpy as jnp
from jax import lax

NT = 1024
NF = 256
NYG = 512
TR_DEV = 1024
ORDER = 8
DEPTHS = 2
OWNERS = 32
TRACES = 32768
NXG = 384
CELLS = 6144
SLOT = 80
N_FREQ = 4


def routing_plan(key):
    folded = jax.random.fold_in(key, 7)
    subkeys = jax.random.split(folded, 7)
    center_tile = jax.random.randint(subkeys[0], (), 0, OWNERS)
    counts = jax.random.randint(subkeys[1], (OWNERS,), TR_DEV // 2, TR_DEV + 1)
    fuller = jax.random.randint(subkeys[2], (), 0, OWNERS)
    counts = jnp.where(jnp.arange(OWNERS) == fuller, TR_DEV, counts).astype(jnp.int32)
    weight = jax.random.randint(subkeys[3], (OWNERS, OWNERS, 1), 1, 5)
    jitter = jax.random.randint(subkeys[4], (OWNERS, OWNERS, SLOT), 0, 1024)
    target = jnp.arange(OWNERS)[None, :, None]
    levels = jitter * weight + jnp.where(target == center_tile, 8192, 0)
    places = OWNERS * SLOT
    flat_score = levels.reshape(OWNERS, places) * places + (places - 1 - jnp.arange(places))[None, :]
    _, chosen = lax.top_k(flat_score, TR_DEV)
    rank_row = jnp.arange(TR_DEV)[None, :]
    shuffle = jax.random.randint(subkeys[5], (OWNERS, TR_DEV), 0, 65536)
    order_key = jnp.where(rank_row < counts[:, None], shuffle * TR_DEV + rank_row, 2 ** 30 + rank_row)
    arrangement = jnp.argsort(order_key, axis=1, stable=True)
    placed = jnp.take_along_axis(chosen, arrangement, axis=1)
    target_tile = placed // SLOT
    within = jax.random.randint(subkeys[6], (OWNERS, TR_DEV), 0, CELLS)
    cell_bins = (target_tile * CELLS + within).reshape(OWNERS * TR_DEV).astype(jnp.int32)
    return (cell_bins, counts)


def draw_bins(key, part):
    return routing_plan(key)[0]


def draw_counts(key, part):
    return routing_plan(key)[1]


def block_levels(key, extent, cuts, low, largest):
    factor_of, own = 1.0, jax.random.fold_in(key, 6)
    for axis_at, blocks in cuts:
        draws = jnp.exp(jax.random.uniform(jax.random.fold_in(own, axis_at), (blocks,), jnp.float32, low / len(cuts), largest / len(cuts)))
        factor_of = factor_of * jnp.repeat(draws, extent[axis_at] // blocks).reshape([-1 if axis == axis_at else 1 for axis in range(len(extent))])
    return factor_of


def gaussian(rng, dims, deviation, limit, cuts=(), held_as=jnp.bfloat16):
    array = deviation * jax.random.normal(rng, dims, jnp.float32)
    if cuts:
        array = array * block_levels(rng, dims, cuts, -0.22, 0.18)
    return jnp.clip(array, -limit, limit).astype(held_as)


def setup_inputs(seed: int = 0) -> dict:
    key_of = jax.random.split(jax.random.key(seed), 6)
    traces = gaussian(key_of[0], (TRACES, NT), 1.0, 6.0, ((0, 32),))
    bins = draw_bins(jax.random.fold_in(key_of[5], 71), 0)
    counts = draw_counts(jax.random.fold_in(key_of[5], 71), 0)
    delay = jnp.clip(0.02 + 0.04 * jax.random.uniform(key_of[3], (DEPTHS, NXG, NYG), jnp.float32) ** block_levels(key_of[3], (DEPTHS, NXG, NYG), ((1, 32),), -0.2, 0.2), 0.02, 0.06)
    coeffs = gaussian(key_of[4], (2, ORDER + 1, NF), 0.35, 1.4, ((2, 4),), jnp.float32)
    return {"traces": traces, "bins": bins, "counts": counts, "delay": delay, "coeffs": coeffs}


def stencil(padded):
    middle = padded[:, :, 1:-1]
    along_x = 0.5 * middle + 0.25 * (padded[:, :, 2:] + padded[:, :, :-2])
    edged = jnp.pad(along_x, ((0, 0), (0, 0), (0, 0), (1, 1)))
    along_y = 0.5 * along_x + 0.25 * (edged[:, :, :, 2:] + edged[:, :, :, :-2])
    return 2.0 * along_y - middle

def apply_operator(field):
    return stencil(jnp.pad(field, ((0, 0), (0, 0), (1, 1), (0, 0))))

def weigh(coef, index, field):
    real_part = coef[0, index][:, None, None]
    imag_part = coef[1, index][:, None, None]
    return jnp.stack([real_part * field[0] - imag_part * field[1], real_part * field[1] + imag_part * field[0]])

def reference(traces, bins, counts, delay, coeffs):
    freq_index = jnp.arange(NF, dtype=jnp.int32) + 1
    turns = jnp.arange(NT, dtype=jnp.int32)[:, None] * freq_index[None, :] % NT
    angle = turns.astype(jnp.float32) * (2.0 * math.pi / NT)
    table = (jnp.concatenate([jnp.cos(angle), -jnp.sin(angle)], axis=1) / math.sqrt(NT)).astype(jnp.bfloat16)
    spectra = jnp.dot(traces, table, preferred_element_type=jnp.float32).astype(jnp.bfloat16)
    alive = (jnp.arange(TR_DEV, dtype=jnp.int32)[None, :] < counts[:, None]).reshape(TRACES)
    values = jnp.where(alive[:, None], spectra.astype(jnp.float32), jnp.float32(0.0))
    stacked = jax.ops.segment_sum(values, bins, num_segments=NXG * NYG)
    field = stacked.reshape(NXG, NYG, 2, NF).transpose(2, 3, 0, 1)
    block = NF // N_FREQ
    field_blocks = field.reshape(2, N_FREQ, block, NXG, NYG).transpose(1, 0, 2, 3, 4)
    coef_blocks = coeffs.reshape(2, ORDER + 1, N_FREQ, block).transpose(2, 0, 1, 3)
    wave_blocks = freq_index.astype(jnp.float32).reshape(N_FREQ, block)

    def migrate(image, pieces):
        wavefield, coef, wave = pieces
        partials = []
        for depth in range(DEPTHS):
            phase = wave[:, None, None] * delay[depth][None]
            cosine = jnp.cos(phase)
            sine = jnp.sin(phase)
            wavefield = jnp.stack([cosine * wavefield[0] - sine * wavefield[1], sine * wavefield[0] + cosine * wavefield[1]])
            total = weigh(coef, 0, wavefield)
            previous = wavefield
            current = apply_operator(wavefield)
            total = total + weigh(coef, 1, current)
            for order in range(2, ORDER + 1):
                upcoming = 2.0 * apply_operator(current) - previous
                previous, current = (current, upcoming)
                total = total + weigh(coef, order, current)
            wavefield = total
            partials.append(lax.optimization_barrier(jnp.sum(total[0], axis=0)) * (1.0 / math.sqrt(NF)))
        return (image + jnp.stack(partials), None)
    image, _ = lax.scan(migrate, jnp.zeros((DEPTHS, NXG, NYG), jnp.float32), (field_blocks, coef_blocks, wave_blocks))
    return image
```

```python
import functools
import math

import jax
import jax.numpy as jnp
import numpy as np
from jax import lax
from jax.experimental import pallas as pl
from jax.experimental.pallas import tpu as pltpu
from jax.sharding import PartitionSpec as P

NF = 256
ORDER = 8
DEPTHS = 2
SLOT = 80
BLOCK = 96
ROWS = 12
HALO = 8
NY = 512
TILES = 32
F32 = jnp.float32
BF16 = jnp.bfloat16
NT_DIMS = (((1,), (1,)), ((), ()))


def sine_basis():
    k = np.arange(1, NY + 1)
    basis = np.sqrt(2.0 / (NY + 1)) * np.sin(np.pi * np.outer(k, k) / (NY + 1))
    high = basis.astype(jnp.bfloat16)
    low = (basis - high.astype(np.float64)).astype(jnp.bfloat16)
    return np.concatenate([high, low], axis=0)


def shift_weights():
    k = np.arange(1, NY + 1)
    s = 0.5 + 0.5 * np.cos(np.pi * k / (NY + 1))
    wide = ORDER + 2

    def apply_g(poly):
        out = (s - 1.0) * poly
        for d in range(wide - 1):
            below = poly[abs(d - 1)]
            out[d] = out[d] + 0.5 * s * (below + poly[d + 1])
        return out

    terms = [np.zeros((wide, NY)) for _ in range(2)]
    terms[0][0] = 1.0
    terms[1] = apply_g(terms[0])
    for _ in range(2, ORDER + 1):
        terms.append(2.0 * apply_g(terms[-1]) - terms[-2])
    return np.stack(terms)[:, : ORDER + 1].astype(np.float32)


def pack_kernel(count_ref, bins_ref, traces_ref, table_ref, out_ref, spec_ref):
    slots = traces_ref.shape[0]
    bins = bins_ref[...]
    tile = ((bins.astype(F32) + 0.5) * (1.0 / (ROWS * NY))).astype(jnp.int32)
    local = bins - tile * (ROWS * NY)
    lane = lax.broadcasted_iota(jnp.int32, (1, slots), 1)
    alive = lane < count_ref[0]
    tile_of = lax.broadcasted_iota(jnp.int32, (TILES, slots), 0)
    hot = (tile_of == jnp.where(alive, tile, -1)).astype(F32)
    before = (
        lax.broadcasted_iota(jnp.int32, (slots, slots), 0)
        < lax.broadcasted_iota(jnp.int32, (slots, slots), 1)
    )
    before = jnp.where(before, 1.0, 0.0).astype(BF16)
    rank = jnp.dot(hot.astype(BF16), before, preferred_element_type=F32)
    place = jnp.sum(hot * (rank + (SLOT * tile_of).astype(F32)), axis=0, keepdims=True)
    place = jnp.where(alive, place.astype(jnp.int32), -1)

    spec_ref[:, :128] = jnp.dot(
        traces_ref[...], table_ref[...], preferred_element_type=F32
    ).astype(BF16)
    kind = lax.broadcasted_iota(jnp.int32, (8, slots), 0)
    code = jnp.where(
        kind == 0, (local >> 9) + 1, jnp.where(kind == 1, local & 255, (local >> 8) & 1)
    )
    code = jnp.where(kind < 3, code, 0).astype(F32)
    spec_ref[:, 128:] = jnp.transpose(jnp.concatenate([code] * 16, axis=0)).astype(BF16)

    group = 8
    lane_group = lax.broadcasted_iota(jnp.int32, (16, 128), 1) >> 3

    def body(step, _):
        base = step * (group * SLOT)
        slot = lax.broadcasted_iota(jnp.int32, (group * SLOT, slots), 0) + base
        pick = jnp.where(slot == place, 1.0, 0.0).astype(BF16)
        got = jnp.dot(pick, spec_ref[...], preferred_element_type=F32)
        for i in range(group):
            dest = step * group + i
            out_ref[dest, 0:SLOT, :] = got[SLOT * i : SLOT * (i + 1), :128].astype(BF16)
            codes = jnp.zeros((16, 128), F32)
            for g in range(5):
                piece = got[SLOT * i + 16 * g : SLOT * i + 16 * (g + 1), 128:]
                codes = jnp.where(lane_group == g, piece, codes)
            out_ref[dest, SLOT:BLOCK, :] = codes.astype(BF16)
        return 0

    lax.fori_loop(0, TILES // group, body, 0)


def pack(counts, bins, traces, table):
    slots = traces.shape[0]
    return pl.pallas_call(
        pack_kernel,
        out_shape=jax.ShapeDtypeStruct((TILES, BLOCK, 128), BF16),
        in_specs=[
            pl.BlockSpec(memory_space=pltpu.SMEM),
            pl.BlockSpec(memory_space=pltpu.VMEM),
            pl.BlockSpec(memory_space=pltpu.VMEM),
            pl.BlockSpec(memory_space=pltpu.VMEM),
        ],
        out_specs=pl.BlockSpec(memory_space=pltpu.VMEM),
        scratch_shapes=[pltpu.VMEM((slots, 256), BF16)],
        cost_estimate=pl.CostEstimate(
            flops=3_000_000_000, bytes_accessed=4_000_000, transcendentals=0
        ),
        compiler_params=pltpu.CompilerParams(vmem_limit_bytes=48 * 1024 * 1024),
        name="pack_traces",
    )(counts, bins.reshape(1, slots), traces, table)


def unpack(recv_ref, vals_ref, hot_ref, code_ref):
    chunk = 8 * SLOT

    def body(step, _):
        lanes = pl.ds(pl.multiple_of(step * chunk, 128), chunk)
        block = recv_ref[pl.ds(step * 8, 8)]
        vals = block[:, :SLOT, :].reshape(chunk, 128).astype(F32)
        vals_ref[:, lanes] = jnp.transpose(vals).astype(BF16)
        codes = block[:, SLOT:BLOCK, :].astype(F32)
        codes = jnp.concatenate([codes] * 5, axis=1).reshape(chunk, 128)
        codes = jnp.transpose(codes)
        k = lax.broadcasted_iota(jnp.int32, (8, chunk), 1)
        owner = ((k.astype(F32) + 0.5) * (1.0 / SLOT)).astype(jnp.int32)
        g_of = (k - owner * SLOT) >> 4
        code = jnp.zeros((8, chunk), F32)
        for g in range(5):
            code = jnp.where(g_of == g, codes[8 * g : 8 * (g + 1)], code)
        code_ref[:, lanes] = code
        y = (code[1:2] + 256.0 * code[2:3]).astype(jnp.int32)
        row = lax.broadcasted_iota(jnp.int32, (NY, chunk), 0)
        hot_ref[:, lanes] = jnp.where(row == y, 1.0, 0.0).astype(BF16)
        return 0

    lax.fori_loop(0, TILES // 8, body, 0)


def spread(lhs_ref, vals_ref, hot_ref, code_ref, first, group):
    for i in range(group):
        mask = jnp.where(code_ref[0:1, :] == (first + (i + 1)).astype(F32), 1.0, 0.0)
        mask = jnp.broadcast_to(mask, (16, mask.shape[1])).astype(BF16)
        lhs_ref[128 * i : 128 * (i + 1), :] = vals_ref[...] * jnp.concatenate([mask] * 8, axis=0)
    return lax.dot_general(lhs_ref[...], hot_ref[...], NT_DIMS, preferred_element_type=F32)


def phase_of(turn_ref, plane, a):
    ac = turn_ref[0, plane, pl.ds(a, 1), :]
    as_ = turn_ref[1, plane, pl.ds(a, 1), :]
    bc = turn_ref[2, plane]
    bs = turn_ref[3, plane]
    return ac * bc - as_ * bs, ac * bs + as_ * bc


def turned(block, turn_ref, plane):
    real, imag = [], []
    for a in range(8):
        wr, wi = phase_of(turn_ref, plane, a)
        re = block[8 * a : 8 * (a + 1)]
        im = block[64 + 8 * a : 64 + 8 * (a + 1)]
        real.append(wr * re - wi * im)
        imag.append(wi * re + wr * im)
    return jnp.concatenate(real + imag, axis=0)


def bin_planes(recv_ref, turn_ref, basis_ref, dst_ref, dst_first, turn_first, x_first, planes, scr):
    vals_ref, hot_ref, code_ref, lhs_ref = scr
    unpack(recv_ref, vals_ref, hot_ref, code_ref)
    group = 4

    def body(step, _):
        out = spread(lhs_ref, vals_ref, hot_ref, code_ref, x_first + step * group, group)
        rows = []
        for i in range(group):
            rows.append(
                turned(out[128 * i : 128 * (i + 1)], turn_ref, turn_first + step * group + i)
            )
        rows = jnp.concatenate(rows, axis=0).astype(BF16)
        res = jnp.dot(rows, basis_ref[:NY], preferred_element_type=F32)
        res = res + jnp.dot(rows, basis_ref[NY:], preferred_element_type=F32)
        for i in range(group):
            dst_ref[dst_first + step * group + i] = res[128 * i : 128 * (i + 1)]
        return 0

    lax.fori_loop(0, planes // group, body, 0)


def own_kernel(recv_ref, turn_ref, basis_ref, out_ref, *scr):
    bin_planes(recv_ref, turn_ref, basis_ref, out_ref, 0, HALO, jnp.int32(0), ROWS, scr)


BIN_SCRATCH = [
    pltpu.VMEM((128, TILES * SLOT), BF16),
    pltpu.VMEM((NY, TILES * SLOT), BF16),
    pltpu.VMEM((8, TILES * SLOT), F32),
    pltpu.VMEM((512, TILES * SLOT), BF16),
]


def own_planes(recv, turn, basis):
    return pl.pallas_call(
        own_kernel,
        out_shape=jax.ShapeDtypeStruct((ROWS, 128, NY), F32),
        in_specs=[pl.BlockSpec(memory_space=pltpu.VMEM)] * 3,
        out_specs=pl.BlockSpec(memory_space=pltpu.VMEM),
        scratch_shapes=BIN_SCRATCH,
        cost_estimate=pl.CostEstimate(
            flops=8_000_000_000, bytes_accessed=8_000_000, transcendentals=0
        ),
        compiler_params=pltpu.CompilerParams(vmem_limit_bytes=56 * 1024 * 1024),
        name="own_planes",
    )(recv, turn, basis)


def main_kernel(
    tile_ref,
    own_ref,
    left_ref,
    right_ref,
    turn_ref,
    basis_ref,
    taps_ref,
    turn1_ref,
    coef_ref,
    flat_ref,
    ext_ref,
    wave_ref,
    mid_ref,
    h_ref,
    *scr,
):
    total = ROWS + 2 * HALO
    tile = tile_ref[0]
    bin_planes(left_ref, turn_ref, basis_ref, wave_ref, 0, 0, jnp.int32(ROWS - HALO), HALO, scr)
    bin_planes(
        right_ref, turn_ref, basis_ref, wave_ref, HALO + ROWS, HALO + ROWS, jnp.int32(0), HALO, scr
    )
    wave_ref[HALO : HALO + ROWS] = own_ref[...]

    @pl.when(tile == 0)
    def _():
        wave_ref[HALO - 1] = jnp.zeros((128, NY), F32)
        for m in range(1, HALO):
            wave_ref[HALO - 1 - m] = -wave_ref[HALO - 1 + m]

    @pl.when(tile == TILES - 1)
    def _():
        edge = HALO + ROWS
        wave_ref[edge] = jnp.zeros((128, NY), F32)
        for m in range(1, HALO):
            wave_ref[edge + m] = -wave_ref[edge - m]

    def taps_body(step, _):
        re_rows = pl.ds(pl.multiple_of(step * 16, 16), 16)
        im_rows = pl.ds(pl.multiple_of(64 + step * 16, 16), 16)
        for lt in range(NY // 128):
            cols = slice(128 * lt, 128 * (lt + 1))
            for x in range(ROWS):
                c = HALO + x
                pr = taps_ref[0, 0, re_rows, cols]
                pi = taps_ref[1, 0, re_rows, cols]
                re = wave_ref[c, re_rows, cols]
                im = wave_ref[c, im_rows, cols]
                acc_r = pr * re - pi * im
                acc_i = pr * im + pi * re
                for d in range(1, HALO + 1):
                    pr = taps_ref[0, d, re_rows, cols]
                    pi = taps_ref[1, d, re_rows, cols]
                    re = wave_ref[c + d, re_rows, cols] + wave_ref[c - d, re_rows, cols]
                    im = wave_ref[c + d, im_rows, cols] + wave_ref[c - d, im_rows, cols]
                    acc_r = acc_r + (pr * re - pi * im)
                    acc_i = acc_i + (pr * im + pi * re)
                mid_ref[x, re_rows, cols] = acc_r.astype(BF16)
                mid_ref[x, im_rows, cols] = acc_i.astype(BF16)
        return 0

    lax.fori_loop(0, 4, taps_body, 0)

    h_ref[...] = jnp.zeros_like(h_ref)
    group = 4

    def depth_body(step, _):
        rows = mid_ref[pl.ds(step * group, group)].reshape(group * 128, NY)
        out = jnp.dot(rows, basis_ref[:NY], preferred_element_type=F32)
        out = out + jnp.dot(rows, basis_ref[NY:], preferred_element_type=F32)
        for i in range(group):
            x = step * group + i
            block = out[128 * i : 128 * (i + 1)]
            flat_ref[pl.ds(x, 1), :] = jnp.sum(block[:64], axis=0, keepdims=True) * (
                1.0 / math.sqrt(NF)
            )
            block = turned(block, turn1_ref, x)
            for n in range(ORDER + 1):
                acc = None
                for s in range(16):
                    w = coef_ref[n, 8 * s : 8 * (s + 1), :]
                    w = jnp.concatenate([w] * 4, axis=1)
                    term = w * block[8 * s : 8 * (s + 1)]
                    acc = term if acc is None else acc + term
                h_ref[n, pl.ds(HALO + x, 1), :] = jnp.sum(acc, axis=0, keepdims=True)
        return 0

    lax.fori_loop(0, ROWS // group, depth_body, 0)

    shape = (32, NY)
    row = lax.broadcasted_iota(jnp.int32, shape, 0)
    col = lax.broadcasted_iota(jnp.int32, shape, 1)
    grid_x = tile * ROWS - HALO + row
    inside = jnp.where((grid_x >= 0) & (grid_x < TILES * ROWS), 1.0, 0.0)
    not_first = col > 0
    not_last = col < NY - 1

    def apply_g(v):
        a = 0.5 * v + 0.25 * (pltpu.roll(v, 1, 0) + pltpu.roll(v, 31, 0))
        left = jnp.where(not_first, pltpu.roll(a, 1, 1), 0.0)
        right = jnp.where(not_last, pltpu.roll(a, NY - 1, 1), 0.0)
        return (a + 0.5 * (left + right) - v) * inside

    after = jnp.zeros(shape, F32)
    current = h_ref[ORDER]
    for n in range(ORDER - 1, 0, -1):
        after, current = current, h_ref[n] + 2.0 * apply_g(current) - after
    ext_ref[...] = (h_ref[0] + apply_g(current) - after) * (1.0 / math.sqrt(NF))


def migrate(tile, own, left, right, turn, basis, taps, turn1, coef):
    vmem = pl.BlockSpec(memory_space=pltpu.VMEM)
    return pl.pallas_call(
        main_kernel,
        out_shape=(
            jax.ShapeDtypeStruct((ROWS, NY), F32),
            jax.ShapeDtypeStruct((32, NY), F32),
        ),
        in_specs=[pl.BlockSpec(memory_space=pltpu.SMEM)] + [vmem] * 8,
        out_specs=(vmem, vmem),
        scratch_shapes=[
            pltpu.VMEM((ROWS + 2 * HALO, 128, NY), F32),
            pltpu.VMEM((ROWS, 128, NY), BF16),
            pltpu.VMEM((ORDER + 1, 32, NY), F32),
        ]
        + BIN_SCRATCH,
        cost_estimate=pl.CostEstimate(
            flops=14_000_000_000, bytes_accessed=12_000_000, transcendentals=0
        ),
        compiler_params=pltpu.CompilerParams(vmem_limit_bytes=60 * 1024 * 1024),
        name="migrate",
    )(tile, own, left, right, turn, basis, taps, turn1, coef)


def times(a, b):
    return a[0] * b[0] - a[1] * b[1], a[0] * b[1] + a[1] * b[0]


def turn_tables(delay, first):
    base_angle = first * delay
    unit = (jnp.cos(delay), jnp.sin(delay))
    powers = [(jnp.ones_like(delay), jnp.zeros_like(delay)), unit]
    for k in range(2, 9):
        powers.append(times(powers[k // 2], powers[k - k // 2]))
    eight = powers[8]
    coarse = [(jnp.cos(base_angle), jnp.sin(base_angle))]
    steps = [None, eight]
    for k in range(2, 8):
        steps.append(times(steps[k // 2], steps[k - k // 2]))
    for a in range(1, 8):
        coarse.append(times(coarse[0], steps[a]))
    fine = powers[:8]
    return jnp.stack(
        [
            jnp.stack([c[0] for c in coarse], axis=1),
            jnp.stack([c[1] for c in coarse], axis=1),
            jnp.stack([c[0] for c in fine], axis=1),
            jnp.stack([c[1] for c in fine], axis=1),
        ]
    )


def per_device(traces, bins, counts, delay, coeffs):
    tile = lax.axis_index("tile")
    freq_dev = coeffs.shape[2]
    samples = traces.shape[1]
    freq_index = lax.axis_index("freq") * freq_dev + jnp.arange(freq_dev, dtype=jnp.int32) + 1
    turns = jnp.arange(samples, dtype=jnp.int32)[:, None] * freq_index[None, :] % samples
    angle = turns.astype(F32) * (2.0 * math.pi / samples)
    table = (
        jnp.concatenate([jnp.cos(angle), -jnp.sin(angle)], axis=1) / math.sqrt(samples)
    ).astype(BF16)

    up = [(i, i + 1) for i in range(TILES - 1)]
    down = [(i + 1, i) for i in range(TILES - 1)]
    above = lax.ppermute(delay[0, ROWS - HALO :], "tile", up)
    below = lax.ppermute(delay[0, :HALO], "tile", down)
    first = (lax.axis_index("freq") * freq_dev + 1).astype(F32)
    turn = turn_tables(jnp.concatenate([above, delay[0], below], axis=0), first)
    turn1 = turn_tables(delay[1], first)

    basis = jnp.asarray(sine_basis())
    weights = jnp.asarray(shift_weights())
    taps = jnp.einsum("cnj,ndk->cdjk", coeffs, weights, precision=lax.Precision.HIGHEST)
    signed = jnp.concatenate([coeffs[0], -coeffs[1]], axis=1)
    coef = jnp.broadcast_to(signed[:, :, None], (ORDER + 1, 2 * freq_dev, 128))

    send = pack(counts, bins, traces, table)
    recv = lax.all_to_all(send, "tile", 0, 0, tiled=True)
    left = lax.ppermute(recv, "tile", up)
    right = lax.ppermute(recv, "tile", down)
    own = own_planes(recv, turn, basis)
    flat, ext = migrate(tile.reshape(1), own, left, right, turn, basis, taps, turn1, coef)

    to_up = lax.ppermute(ext[HALO + ROWS : ROWS + 2 * HALO], "tile", up)
    to_down = lax.ppermute(ext[:HALO], "tile", down)
    pad = ((0, ROWS - HALO), (0, 0))
    image = ext[HALO : HALO + ROWS] + jnp.pad(to_up, pad) + jnp.pad(to_down, ((ROWS - HALO, 0), (0, 0)))
    partial = jnp.stack([flat, image])
    count = lax.axis_size("freq")
    blocks = partial.reshape(DEPTHS, ROWS, count, NY // count).transpose(2, 0, 1, 3)
    return jnp.sum(lax.all_to_all(blocks, "freq", 0, 0, tiled=True), axis=0)


def solution(mesh):
    in_specs = (P("tile", None), P("tile"), P("tile"), P(None, "tile", None), P(None, None, "freq"))
    out_specs = P(None, "tile", "freq")
    return jax.shard_map(
        per_device, mesh=mesh, in_specs=in_specs, out_specs=out_specs, check_vma=False
    )
```
